256 devices in a mesh: grp: 32 (over x, z_hi, y), ep: 8 (over z_lo, core).
Axes of the slice: x: 4, y: 4, z: 8 (z_hi: 2, z_lo: 4; z = z_hi * 4 + z_lo), core: 2. Of those that a mesh axis runs over, the one named last changes fastest.
Arguments:
- queries: bfloat16 [1024, 2304], P('grp'), may hold values from -36 to 36, as said below
- residual: bfloat16 [1024, 2304], P(('grp', 'ep')), may hold values from -20 to 20
- gain: bfloat16 [2304], replicated, may hold values from 0.5 to 1.5
- key_pages: bfloat16 [2048, 128, 2304], P(('grp', 'ep')), may hold values from -6 to 6
- value_pages: bfloat16 [2048, 128, 2304], P(('grp', 'ep')), may hold values from -6 to 6
- page_table: int32 [1024, 32], P('grp'), may hold values from -1 to 63, as said below
- lengths: int32 [1024], P('grp'), may hold values from 1 to 4096, as said below
- split_flag: int32 [1024], P('grp'), may hold values from 0 to 1, as said below
- routes: int32 [1024, 2], P(('grp', 'ep')), may hold values from 0 to 7, all different within a row; in each aligned block of 4 rows (0 to 3, 4 to 7, ...) at most 2 rows name the same one
- gates: bfloat16 [1024, 2], P(('grp', 'ep')), may hold values from 0.19921875 to 1
- w_gate: bfloat16 [8, 2304, 5760], P('ep', None, 'grp'), may hold values from -0.125 to 0.125
- w_up: bfloat16 [8, 2304, 5760], P('ep', None, 'grp'), may hold values from -0.125 to 0.125
- w_down: bfloat16 [8, 5760, 2304], P('ep', 'grp'), may hold values from -0.078125 to 0.078125
Outputs:
- update: bfloat16 [1024, 2304], P(('grp', 'ep'))
The draws below stay inside these ranges and needn't reach their ends.
Inputs may be any that keep to these rules, and one draw needn't show every extreme that they name: `page_table`: entries j with j * 128 < lengths[r] are pages of the row's group; no page is named twice within a group; the other entries are -1. `lengths`: A split request's first half, in the even group of its pair, is always 32 * 128 tokens; other rows are no longer. `split_flag`: in every group exactly one row is 1, at the same slot in both groups of each pair 2i, 2i + 1. `routes`: within the rows of one device no expert is named more than 2 times. `queries`: the two rows of a split request hold the same query.
All inputs are finite; a program needn't handle non-finite values.
Results may differ from the reference program's by a relative error of at most 0.015.
Values may be sent and summed in bfloat16 or wider, within the bound.
No kernel may reach another device: no remote copies, remote signals or barrier semaphores. Data moves between devices by JAX's collectives and lax.ppermute only.
A program may use at most 192 MiB of HBM per device.

```python
import math
import jax
import jax.numpy as jnp
import numpy as np
from jax import lax

HEADS = 36
HEAD_DIM = 64
D = 2304
FF = 5760
EXPERTS = 8
PAGE = 128
REQ_DEV = 4
PAGES_DEV = 8
LONG_PAGES = 32
CAP = 2
ROWS = 1024
PAGES_ALL = 2048
N_GRP = 32
N_EP = 8


def layout_draw(key):
    pair_count = N_GRP // 2
    pool_size = PAGES_DEV * N_EP
    group_rows = REQ_DEV * N_EP
    split_slot = jax.random.randint(jax.random.fold_in(key, 11), (pair_count,), 0, group_rows).astype(jnp.int32)
    tail_length = jax.random.randint(jax.random.fold_in(key, 12), (pair_count,), 1, LONG_PAGES * PAGE + 1).astype(jnp.int32)
    short_length = jax.random.randint(jax.random.fold_in(key, 13), (N_GRP, group_rows), 1, PAGE + 1).astype(jnp.int32)
    group_keys = jax.random.split(jax.random.fold_in(key, 14), N_GRP)
    orders = jax.vmap(lambda group_key: jax.random.permutation(group_key, pool_size))(group_keys).astype(jnp.int32)
    first_entry = orders[:, :1]
    orders = jnp.where(orders == pool_size - 1, first_entry, orders)
    column_ids = jnp.arange(pool_size, dtype=jnp.int32)
    orders = jnp.where(column_ids[None, :] == 0, pool_size - 1, orders).astype(jnp.int32)
    group_ids = jnp.arange(N_GRP, dtype=jnp.int32)
    slot_ids = jnp.arange(group_rows, dtype=jnp.int32)
    chosen = split_slot[group_ids // 2]
    is_split = slot_ids[None, :] == chosen[:, None]
    is_odd = (group_ids % 2 == 1)[:, None]
    long_length = jnp.where(is_odd, tail_length[group_ids // 2][:, None], LONG_PAGES * PAGE)
    row_lengths = jnp.where(is_split, long_length, short_length).astype(jnp.int32)
    ranking = slot_ids[None, :] - (slot_ids[None, :] > chosen[:, None]).astype(jnp.int32)
    short_page = jnp.take_along_axis(orders, LONG_PAGES + ranking, axis=1)
    table_steps = jnp.arange(LONG_PAGES, dtype=jnp.int32)
    long_pages = orders[:, :LONG_PAGES]
    short_rows = jnp.where(table_steps[None, None, :] == 0, short_page[:, :, None], -1)
    page_rows = jnp.where(is_split[:, :, None], long_pages[:, None, :], short_rows)
    live_step = table_steps[None, None, :] * PAGE < row_lengths[:, :, None]
    page_rows = jnp.where(live_step, page_rows, -1).astype(jnp.int32)
    return (page_rows.reshape(ROWS, LONG_PAGES), row_lengths.reshape(ROWS), is_split.astype(jnp.int32).reshape(ROWS))


def draw_page_table(key, part):
    return layout_draw(key)[0]


def draw_lengths(key, part):
    return layout_draw(key)[1]


def draw_split_flag(key, part):
    return layout_draw(key)[2]


def draw_queries(key, part):
    base = jax.random.normal(jax.random.fold_in(key, 1), (ROWS, D), jnp.float32)
    base = jnp.clip(base, -36.0, 36.0)
    split_rows = layout_draw(key)[2]
    grouped = base.reshape(N_GRP // 2, 2, REQ_DEV * N_EP, D)
    flags = split_rows.reshape(N_GRP // 2, 2, REQ_DEV * N_EP)[:, 1]
    second = jnp.where(flags[..., None] == 1, grouped[:, 0], grouped[:, 1])
    joined = jnp.stack([grouped[:, 0], second], axis=1)
    return joined.reshape(ROWS, D).astype(jnp.bfloat16)


def draw_key_pages(key, part):
    base = jax.random.normal(jax.random.fold_in(key, 2), (PAGES_ALL, PAGE, D), jnp.float32)
    return jnp.clip(base, -6.0, 6.0).astype(jnp.bfloat16)


def draw_residual(key, part):
    row_scale = jnp.exp(jax.random.uniform(jax.random.fold_in(key, 21), (ROWS, 1), jnp.float32, jnp.log(0.3), jnp.log(3.0)))
    col_scale = jnp.exp(jax.random.uniform(jax.random.fold_in(key, 22), (1, D), jnp.float32, jnp.log(0.5), jnp.log(2.0)))
    base = jax.random.normal(jax.random.fold_in(key, 23), (ROWS, D), jnp.float32)
    return jnp.clip(base * row_scale * col_scale, -20.0, 20.0).astype(jnp.bfloat16)


def block_scale(own_key, extent, pieces, smallest, top_value):
    def one(axis_at, blocks):
        draws = jax.random.uniform(jax.random.fold_in(jax.random.fold_in(own_key, 6), axis_at), (blocks,), jnp.float32, smallest / len(pieces), top_value / len(pieces))
        return jnp.repeat(jnp.exp(draws), extent[axis_at] // blocks).reshape((-1,) + (1,) * (len(extent) - axis_at - 1))

    factor_of = one(*pieces[0])
    for cut in pieces[1:]:
        factor_of = factor_of * one(*cut)
    return factor_of


def shared_out(stream_key, own, number, rows, number_of, top, bound, slope):
    order = jax.random.permutation(stream_key, number_of)
    heavy_load, usual = load_shares(number_of, rows * top, bound, slope, True), load_shares(number_of, rows * top, bound, slope, False)
    places = jnp.arange(number_of)

    def named(sizes, turn):
        used = int((sizes > 0).sum())
        fixed = max(1, used // 4)
        passed = fixed + (places - fixed + turn * (used - fixed)) % max(1, number_of - fixed)
        return jnp.zeros((number_of,), jnp.int32).at[order[jnp.where(places < fixed, places, passed)]].set(jnp.asarray(sizes, jnp.int32))

    sizes = jnp.where(number % 4 == 0, named(heavy_load, number // 4), named(usual, number - number // 4 - 1))
    mixed = jax.random.permutation(jax.random.fold_in(own, 3), number_of)
    donor, receiver = mixed[0:number_of // 2 * 2:2], mixed[1:number_of // 2 * 2:2]
    slack = jnp.minimum(sizes[donor] - 1, bound - sizes[receiver]) // 2
    slack = jnp.where((donor == order[0]) | (receiver == order[0]) | (sizes[receiver] == 0), 0, jnp.maximum(slack, 0))
    passed = jax.random.randint(jax.random.fold_in(own, 4), (number_of // 2,), 0, 1 << 20) % (slack + 1)
    sizes = sizes.at[donor].add(-passed).at[receiver].add(passed)
    members = jnp.searchsorted(jnp.cumsum(sizes), jnp.arange(rows * top), side="right").astype(jnp.int32)
    listing = members.reshape(top, rows).T
    listing = listing[jax.random.permutation(jax.random.fold_in(own, 1), rows)]
    turn = jax.random.randint(jax.random.fold_in(own, 2), (rows, 1), 0, top)
    return jnp.take_along_axis(listing, (jnp.arange(top)[None, :] + turn) % top, axis=1)


def load_shares(amount, total, limit, skew, full):
    weights = [(1 << 20) // math.isqrt(rank ** skew) + 1 for rank in range(1, amount + 1)]
    largest = limit if full else min(limit, max(-(-total // amount), total * weights[0] // sum(weights)))
    least = 1 if total - largest >= amount - 1 else 0
    given, rest = [largest] + [least] * (amount - 1), total - largest - least * (amount - 1)
    while rest > 0:
        candidates = [i for i in range(1, amount) if given[i] < largest] or [i for i in range(1, amount) if given[i] < limit]
        pool, remaining = sum([weights[i] for i in candidates]), rest
        for i in candidates:
            extra = min(limit - given[i], max(1, remaining * weights[i] // pool), rest)
            given[i] = given[i] + extra
            rest = rest - extra
    return np.array(given)


def centred(rng, shape, scale, limit, cuts=(), kind=jnp.bfloat16):
    result = scale * jax.random.normal(rng, shape, jnp.float32)
    if cuts:
        result = result * block_scale(rng, shape, cuts, -0.22, 0.18)
    return jnp.clip(result, -limit, limit).astype(kind)


def setup_inputs(seed: int = 0) -> dict:
    splits = jax.random.split(jax.random.key(seed), 14)
    queries = draw_queries(jax.random.fold_in(splits[13], 71), 0)
    residual = draw_residual(jax.random.fold_in(splits[13], 71), 0)
    gain = jnp.clip(1.0 + 0.1 * jax.random.normal(splits[2], (D,), jnp.float32), 0.5, 1.5).astype(jnp.bfloat16)
    key_pages = draw_key_pages(jax.random.fold_in(splits[13], 71), 0)
    value_pages = centred(splits[4], (PAGES_ALL, PAGE, D), 1.0, 6.0, ((0, 256),))
    page_table = draw_page_table(jax.random.fold_in(splits[13], 71), 0)
    lengths = draw_lengths(jax.random.fold_in(splits[13], 71), 0)
    split_flag = draw_split_flag(jax.random.fold_in(splits[13], 71), 0)
    routes_keys = jax.random.split(jax.random.fold_in(splits[8], 1), ROWS // REQ_DEV)
    routes_turns = jax.random.permutation(jax.random.fold_in(splits[8], 3), ROWS // REQ_DEV)
    routes = jax.vmap(lambda own, number: shared_out(jax.random.fold_in(splits[8], 2), own, number, REQ_DEV, EXPERTS, 2, CAP, 2))(routes_keys, routes_turns).reshape((ROWS, 2))
    gates = jnp.clip(0.19921875 + 0.80078125 * jax.random.uniform(splits[9], (ROWS, 2), jnp.float32) ** block_scale(splits[9], (ROWS, 2), ((0, 256),), -0.2, 0.2), 0.19921875, 1.0).astype(jnp.bfloat16)
    w_gate = centred(splits[10], (EXPERTS, D, FF), D ** -0.5, 0.125, ((0, 8), (2, 32)))
    w_up = centred(splits[11], (EXPERTS, D, FF), D ** -0.5, 0.125, ((0, 8), (2, 32)))
    w_down = centred(splits[12], (EXPERTS, FF, D), FF ** -0.5, 0.078125, ((0, 8), (1, 32)))
    return {"queries": queries, "residual": residual, "gain": gain, "key_pages": key_pages, "value_pages": value_pages, "page_table": page_table, "lengths": lengths, "split_flag": split_flag, "routes": routes, "gates": gates, "w_gate": w_gate, "w_up": w_up, "w_down": w_down}


NEG_FILL = -1e+30
NORM_EPS = 1e-06

def merge_parts(first_part, second_part):
    maxima_a, totals_a, weighted_a = first_part
    maxima_b, totals_b, weighted_b = second_part
    highest = jnp.maximum(maxima_a, maxima_b)
    factor_a = jnp.exp(maxima_a - highest)
    factor_b = jnp.exp(maxima_b - highest)
    head_count = maxima_a.shape[-1]
    shaped = weighted_a.shape
    wide = shaped[:-1] + (head_count, shaped[-1] // head_count)
    weighted = weighted_a.reshape(wide) * factor_a[..., None] + weighted_b.reshape(wide) * factor_b[..., None]
    return (highest, totals_a * factor_a + totals_b * factor_b, weighted.reshape(shaped))

def page_partials(group_q, page_rows, row_lengths, key_rows, value_rows, first_page):
    page_count = key_rows.shape[0]
    slot_count = group_q.shape[0]
    head_count = group_q.shape[1] // HEAD_DIM
    page_ids = first_page + jnp.arange(page_count, dtype=jnp.int32)
    table_steps = jnp.arange(page_rows.shape[1], dtype=jnp.int32)
    live_step = (table_steps * PAGE)[None, :] < row_lengths[:, None]
    matches = (page_rows[:, :, None] == page_ids[None, None, :]) & live_step[:, :, None]
    owned_page = jnp.any(matches, axis=1)
    where_at = lax.optimization_barrier(jnp.sum(jnp.where(matches, table_steps[None, :, None], 0), axis=1))
    offsets = jnp.arange(PAGE, dtype=jnp.int32)
    token_pos = where_at[:, :, None] * PAGE + offsets[None, None, :]
    visible = (owned_page[:, :, None] & (token_pos < row_lengths[:, None, None])).reshape(slot_count, page_count * PAGE)
    query_heads = group_q.reshape(slot_count, head_count, HEAD_DIM).astype(jnp.float32)
    key_heads = key_rows.reshape(page_count * PAGE, head_count, HEAD_DIM).astype(jnp.float32)
    value_heads = value_rows.reshape(page_count * PAGE, head_count, HEAD_DIM).astype(jnp.float32)
    scores = jnp.einsum('shd,khd->hsk', query_heads, key_heads) * HEAD_DIM ** (-0.5)
    scores = jnp.where(visible[None], scores, NEG_FILL)
    maxima = lax.optimization_barrier(jnp.max(scores, axis=2))
    exp_terms = jnp.where(visible[None], jnp.exp(scores - maxima[..., None]), 0.0)
    totals = lax.optimization_barrier(jnp.sum(exp_terms, axis=2))
    weights = exp_terms.astype(jnp.bfloat16)
    weighted = jnp.einsum('hsk,khd->shd', weights.astype(jnp.float32), value_heads)
    return (maxima.T, totals.T, weighted.reshape(slot_count, head_count * HEAD_DIM))

def flip_pairs(array):
    return array.reshape((N_GRP // 2, 2) + array.shape[1:])[:, ::-1].reshape(array.shape)

def reference(queries, residual, gain, key_pages, value_pages, page_table, lengths, split_flag, routes, gates, w_gate, w_up, w_down):
    pool_size = PAGES_DEV * N_EP
    group_rows = REQ_DEV * N_EP

    def one_group(inputs):
        group_q, page_rows, row_lengths, key_rows, value_rows = inputs
        return page_partials(group_q, page_rows, row_lengths, key_rows, value_rows, 0)
    maxima, totals, weighted = lax.map(one_group, (queries.reshape(N_GRP, group_rows, D), page_table.reshape(N_GRP, group_rows, LONG_PAGES), lengths.reshape(N_GRP, group_rows), key_pages.reshape(N_GRP, pool_size, PAGE, D), value_pages.reshape(N_GRP, pool_size, PAGE, D)))
    joined = merge_parts((maxima, totals, weighted), (flip_pairs(maxima), flip_pairs(totals), flip_pairs(weighted)))
    is_split = (split_flag.reshape(N_GRP, group_rows) == 1)[..., None]
    totals = jnp.where(is_split, joined[1], totals)
    weighted = jnp.where(is_split, joined[2], weighted)
    attn = (weighted.reshape(N_GRP, group_rows, HEADS, HEAD_DIM) / totals[..., None]).reshape(ROWS, D).astype(jnp.bfloat16)
    stream = residual.astype(jnp.float32) + attn.astype(jnp.float32)
    normed = (stream * lax.rsqrt(lax.optimization_barrier(jnp.mean(stream * stream, axis=-1, keepdims=True)) + NORM_EPS) * gain.astype(jnp.float32)).astype(jnp.bfloat16)
    device_count = N_GRP * N_EP
    expert_count = N_EP
    slot_count = expert_count * CAP
    chosen = routes.reshape(device_count, REQ_DEV * 2)
    one_hot = (chosen[:, :, None] == jnp.arange(expert_count, dtype=jnp.int32)[None, None, :]).astype(jnp.int32)
    ranking = lax.optimization_barrier(jnp.sum((jnp.cumsum(one_hot, axis=1) - one_hot) * one_hot, axis=2))
    slot_of = chosen * CAP + ranking
    slot_ids = jnp.arange(slot_count, dtype=jnp.int32)
    placing = (slot_ids[None, :, None] == slot_of[:, None, :]).astype(jnp.float32)
    doubled = jnp.repeat(normed.reshape(device_count, REQ_DEV, D), 2, axis=1).astype(jnp.float32)
    outgoing = jnp.einsum('dca,dae->dce', placing, doubled).astype(jnp.bfloat16)
    expert_inputs = outgoing.reshape(device_count, expert_count, CAP, D).transpose(1, 0, 2, 3).reshape(expert_count, device_count * CAP, D)

    def expert_out(inputs):
        rows_in, gate_matrix, up_matrix, down_matrix = inputs
        gate_part = jnp.dot(rows_in, gate_matrix, preferred_element_type=jnp.float32)
        up_part = jnp.dot(rows_in, up_matrix, preferred_element_type=jnp.float32)
        inner = (jax.nn.silu(gate_part) * up_part).astype(jnp.bfloat16)
        return jnp.dot(inner, down_matrix, preferred_element_type=jnp.float32).astype(jnp.bfloat16)
    results = lax.map(expert_out, (expert_inputs, w_gate, w_up, w_down))
    returned = results.reshape(expert_count, device_count, CAP, D).transpose(1, 0, 2, 3).reshape(device_count, slot_count, D)
    picking = (slot_of[:, :, None] == slot_ids[None, None, :]).astype(jnp.float32) * gates.reshape(device_count, REQ_DEV * 2)[:, :, None].astype(jnp.float32)
    blending = picking.reshape(device_count, REQ_DEV, 2, slot_count).sum(axis=2).astype(jnp.bfloat16)
    mixture = jnp.einsum('drc,dce->dre', blending.astype(jnp.float32), returned.astype(jnp.float32)).reshape(ROWS, D)
    return (attn.astype(jnp.float32) + mixture).astype(jnp.bfloat16)
```

```python
import jax
import jax.numpy as jnp
from jax import lax
from jax.experimental import pallas as pl
from jax.experimental.pallas import tpu as pltpu
from jax.sharding import Mesh, PartitionSpec as P

HEADS = 36
HEAD_DIM = 64
PAGE = 128
D = HEADS * HEAD_DIM
HP = 48
LW = 128
W = D + LW
NEG_FILL = -1e30
NORM_EPS = 1e-06
F32 = jnp.float32
BF16 = jnp.bfloat16


def dot(a, b, ca=1, cb=0):
    return lax.dot_general(a, b, (((ca,), (cb,)), ((), ())), preferred_element_type=F32)


def head_mask(rows, cols):
    row = lax.broadcasted_iota(jnp.int32, (rows, cols), 0)
    col = lax.broadcasted_iota(jnp.int32, (rows, cols), 1)
    return (col >= row * HEAD_DIM) & (col < (row + 1) * HEAD_DIM)


def placed(part, shape, axis):
    head = lax.broadcasted_iota(jnp.int32, shape, axis)
    lane = lax.broadcasted_iota(jnp.int32, shape, 1 - axis)
    return ((lane == head + part * HEADS) & (head < HEADS)).astype(BF16)


def halves(value):
    high = value.astype(BF16)
    return high, (value - high.astype(F32)).astype(BF16)


def attn_kernel(first_ref, q_ref, table_ref, len_ref, k_hbm, v_hbm, out_ref, kbuf, vbuf, obuf, ksem, vsem):
    pages = k_hbm.shape[0]
    rows = q_ref.shape[0]
    for p in range(pages):
        pltpu.make_async_copy(k_hbm.at[p], kbuf.at[p], ksem.at[p]).start()
        pltpu.make_async_copy(v_hbm.at[p], vbuf.at[p], vsem.at[p]).start()
    first = first_ref[0]
    table = table_ref[...]
    length = len_ref[...]
    start = lax.broadcasted_iota(jnp.int32, table.shape, 1) * PAGE
    remain = jnp.clip(length - start, 0, PAGE)
    lane = lax.broadcasted_iota(jnp.int32, (rows, pages), 1)
    owner = jnp.zeros((rows, pages), F32)
    seen = []
    for p in range(pages):
        match = jnp.where(table == first + p, remain, 0).astype(F32)
        per_row = jnp.sum(match, axis=1, keepdims=True)
        seen.append(jnp.sum(per_row, axis=0, keepdims=True).astype(jnp.int32))
        owner = jnp.where((lane == p) & (per_row > 0), 1.0, owner)
    owner_b = owner.astype(BF16)
    q_sel = dot(owner_b, q_ref[...], 0, 0)
    mask = head_mask(HP, D)
    spread = mask.astype(F32).astype(BF16)
    token = lax.broadcasted_iota(jnp.int32, (PAGE, HP), 0)
    tops, sums = [], []
    for p in range(pages):
        q_diag = jnp.where(mask, q_sel[p : p + 1, :], 0.0).astype(BF16)
        pltpu.make_async_copy(k_hbm.at[p], kbuf.at[p], ksem.at[p]).wait()
        scores = dot(kbuf[p], q_diag, 1, 1) * HEAD_DIM**-0.5
        visible = token < seen[p]
        scores = jnp.where(visible, scores, NEG_FILL)
        top = jnp.max(scores, axis=0, keepdims=True)
        terms = jnp.where(visible, jnp.exp(scores - top), 0.0)
        tops.append(top)
        sums.append(jnp.sum(terms, axis=0, keepdims=True))
        pltpu.make_async_copy(v_hbm.at[p], vbuf.at[p], vsem.at[p]).wait()
        mixed = dot(terms.astype(BF16), vbuf[p], 0, 0)
        obuf[p : p + 1, :] = jnp.sum(jnp.where(mask, mixed, 0.0), axis=0, keepdims=True)
    top = jnp.concatenate(tops, axis=0)
    total = jnp.concatenate(sums, axis=0)
    total = jnp.where(total > 0, total, 1.0)
    lse = top + jnp.log(total)
    same = dot(owner_b, owner_b, 0, 0)
    peak = jnp.full(lse.shape, NEG_FILL, F32)
    for p in range(pages):
        peak = jnp.maximum(peak, jnp.where(same[:, p : p + 1] > 0, lse[p : p + 1, :], NEG_FILL))
    share = jnp.exp(lse - peak)
    whole = jnp.zeros(lse.shape, F32)
    for p in range(pages):
        whole = whole + jnp.where(same[:, p : p + 1] > 0, share[p : p + 1, :], 0.0)
    whole = jnp.where(whole > 0, whole, 1.0)
    high, low = halves(share / (whole * total))
    scaled = (dot(high, spread) + dot(low, spread)) * obuf[...]
    high, low = halves(scaled)
    out_ref[:, :D] = (dot(owner_b, high) + dot(owner_b, low)).astype(BF16)
    joint = peak + jnp.log(whole)
    row_lse = jnp.full((rows, HP), NEG_FILL, F32)
    for p in range(pages):
        row_lse = jnp.maximum(row_lse, jnp.where(owner[:, p : p + 1] > 0, joint[p : p + 1, :], NEG_FILL))
    first_part, rest = row_lse.astype(BF16), None
    rest = row_lse - first_part.astype(F32)
    second, third = halves(rest)
    packed = (
        dot(first_part, placed(0, (HP, LW), 0))
        + dot(second, placed(1, (HP, LW), 0))
        + dot(third, placed(2, (HP, LW), 0))
    )
    out_ref[:, D:] = packed.astype(BF16)


def merge_kernel(arr_ref, valid_ref, res_ref, gain_ref, coef_ref, attn_ref, out_ref):
    own = res_ref.shape[0]
    count = arr_ref.shape[0] // own
    folded = placed(0, (LW, HP), 1) + placed(1, (LW, HP), 1) + placed(2, (LW, HP), 1)
    lse = dot(arr_ref[:, D:], folded)
    lse = jnp.where(valid_ref[...] > 0, lse, NEG_FILL)
    parts = [lse[own * s : own * (s + 1), :] for s in range(count)]
    peak = parts[0]
    for part in parts[1:]:
        peak = jnp.maximum(peak, part)
    shares = [jnp.exp(part - peak) for part in parts]
    whole = shares[0]
    for share in shares[1:]:
        whole = whole + share
    scale = 1.0 / whole
    weight = jnp.concatenate([share * scale for share in shares], axis=0)
    spread = head_mask(HP, D).astype(F32).astype(BF16)
    high, low = halves(weight)
    scaled = (dot(high, spread) + dot(low, spread)) * arr_ref[:, :D].astype(F32)
    row = lax.broadcasted_iota(jnp.int32, (own, own * count), 0)
    col = lax.broadcasted_iota(jnp.int32, (own, own * count), 1)
    gather = (lax.rem(col, own) == row).astype(BF16)
    high, low = halves(scaled)
    attn = (dot(gather, high) + dot(gather, low)).astype(BF16)
    attn_ref[...] = attn
    stream = res_ref[...].astype(F32) + attn.astype(F32)
    normed = (
        stream
        * lax.rsqrt(jnp.mean(stream * stream, axis=-1, keepdims=True) + NORM_EPS)
        * gain_ref[...].astype(F32)
    ).astype(BF16)
    for i in range(out_ref.shape[0] // own):
        out_ref[own * i : own * (i + 1), :D] = normed
        out_ref[own * i : own * (i + 1), D:] = coef_ref[...]


def mlp_kernel(count, expert_ref, *refs):
    blocks = refs[:count]
    gate_0, up_0, down_0, gate_1, up_1, down_1 = refs[count : count + 6]
    outs = refs[count + 6 :]
    rows = blocks[0].shape[0]
    each = count // 2
    for half in range(2):
        mine = [ref[...] for ref in blocks[half * each : (half + 1) * each]]
        joined = jnp.concatenate(mine, axis=0)
        x = joined[:, :D]
        coefs = joined[:, D:].astype(F32)
        lane = lax.broadcasted_iota(jnp.int32, coefs.shape, 1)
        result = None
        for k, (gate, up, down) in enumerate(((gate_0, up_0, down_0), (gate_1, up_1, down_1))):
            coef = jnp.sum(jnp.where(lane == expert_ref[k], coefs, 0.0), axis=1, keepdims=True)
            g = dot(x, gate[...])
            u = dot(x, up[...])
            inner = ((g / (1.0 + jnp.exp(-g))) * u * coef).astype(BF16)
            y = dot(inner, down[...])
            result = y if result is None else result + y
        result = result.astype(BF16)
        for i in range(each):
            outs[half * each + i][...] = result[rows * i : rows * (i + 1), :]


VMEM = pltpu.CompilerParams(vmem_limit_bytes=56 * 1024 * 1024)
X = "x"
Y = ("yh", "yp")
Z = ("zh", "zl")


def shifted(array, axis, shift, n=4):
    return lax.ppermute(array, axis, [(i, (i + shift) % n) for i in range(n)])


def gathered(array, axis):
    return [array] + [shifted(array, axis, s) for s in (1, 2, 3)]


def scattered(blocks, axis):
    back = [shifted(block, axis, -s) for s, block in zip((1, 2, 3), blocks[1:])]
    total = blocks[0].astype(F32)
    for block in back:
        total = total + block.astype(F32)
    return total.astype(BF16)


def on_device(
    queries, residual, gain, key_pages, value_pages, page_table, lengths, split_flag, routes, gates,
    w_gate, w_up, w_down,
):
    own = residual.shape[0]
    rows = queries.shape[0]
    pages = key_pages.shape[0]
    my_ep = lax.axis_index(("zl", "c"))
    my_pair = lax.axis_index("yp")
    swap = [(0, 1), (1, 0)]
    mine = (w_gate[0], w_up[0], w_down[0])
    theirs = tuple(lax.ppermute(w, "c", swap) for w in mine)
    experts = jnp.stack([my_ep, my_ep ^ 1]).astype(jnp.int32)

    partial = pl.pallas_call(
        attn_kernel,
        out_shape=jax.ShapeDtypeStruct((rows, W), BF16),
        in_specs=[pl.BlockSpec(memory_space=pltpu.SMEM)]
        + [pl.BlockSpec(memory_space=pltpu.VMEM)] * 3
        + [pl.BlockSpec(memory_space=pl.ANY)] * 2,
        scratch_shapes=[
            pltpu.VMEM((pages, PAGE, D), BF16),
            pltpu.VMEM((pages, PAGE, D), BF16),
            pltpu.VMEM((pages, D), F32),
            pltpu.SemaphoreType.DMA((pages,)),
            pltpu.SemaphoreType.DMA((pages,)),
        ],
        compiler_params=VMEM,
        name="attn",
    )(
        (my_ep * pages).astype(jnp.int32).reshape(1), queries, page_table, lengths.reshape(rows, 1),
        key_pages, value_pages,
    )
    both = jnp.concatenate([partial, partial], axis=0)
    arrived = lax.all_to_all(both, ("yp", "zl", "c"), 0, 0, tiled=True)
    sources = arrived.shape[0] // own
    split_own = lax.dynamic_slice_in_dim(split_flag, my_ep * own, own, 0) == 1
    same_group = (jnp.arange(sources) // (sources // 2)) == my_pair
    valid = (same_group[:, None] | split_own[None, :]).astype(F32).reshape(sources * own, 1)
    lanes = jnp.arange(LW, dtype=jnp.int32)
    coefs = jnp.sum(
        jnp.where(routes[:, :, None] == lanes[None, None, :], gates[:, :, None].astype(F32), 0.0), axis=1
    ).astype(BF16)
    attn, normed = pl.pallas_call(
        merge_kernel,
        out_shape=(
            jax.ShapeDtypeStruct((own, D), BF16),
            jax.ShapeDtypeStruct((8 * own, W), BF16),
        ),
        compiler_params=VMEM,
        name="merge",
    )(arrived, valid, residual, gain.reshape(1, D), coefs)

    stacked = lax.all_to_all(normed, Z, 0, 0, tiled=True)
    half = stacked.shape[0] // 2
    a_x = jnp.concatenate(gathered(stacked[:half], X), axis=0)
    b_y = jnp.concatenate(gathered(stacked[half:], Y), axis=0)
    a_all = gathered(a_x, Y)
    b_all = gathered(b_y, X)
    blocks = a_all + b_all
    results = pl.pallas_call(
        lambda *refs: mlp_kernel(len(blocks), *refs),
        out_shape=[jax.ShapeDtypeStruct((4 * half, D), BF16)] * len(blocks),
        in_specs=[pl.BlockSpec(memory_space=pltpu.SMEM)]
        + [pl.BlockSpec(memory_space=pltpu.VMEM)] * (len(blocks) + 6),
        compiler_params=VMEM,
        name="mlp",
    )(experts, *blocks, *mine, *theirs)
    a_back = scattered(results[:4], Y)
    b_back = scattered(results[4:], X)
    a_fin = scattered([a_back[half * i : half * (i + 1)] for i in range(4)], X)
    b_fin = scattered([b_back[half * i : half * (i + 1)] for i in range(4)], Y)
    outgoing = jnp.concatenate([a_fin, b_fin], axis=0)
    returned = lax.all_to_all(outgoing, Z, 0, 0, tiled=True).reshape(-1, own, D)
    mixture = jnp.sum(returned.astype(F32), axis=0)
    return (attn.astype(F32) + mixture).astype(BF16)


def solution(mesh):
    fine = Mesh(mesh.devices.reshape(4, 2, 2, 2, 4, 2), ("x", "zh", "yh", "yp", "zl", "c"))
    grp = ("x", "zh", "yh", "yp")
    ep = ("zl", "c")
    in_specs = (
        P(grp, None),
        P(grp + ep, None),
        P(),
        P(grp + ep, None, None),
        P(grp + ep, None, None),
        P(grp, None),
        P(grp),
        P(grp),
        P(grp + ep, None),
        P(grp + ep, None),
        P(ep, None, grp),
        P(ep, None, grp),
        P(ep, grp, None),
    )
    return jax.shard_map(
        on_device, mesh=fine, in_specs=in_specs, out_specs=P(grp + ep, None), check_vma=False
    )
```

```python
import jax
import jax.numpy as jnp
from jax import lax
from jax.experimental import pallas as pl
from jax.experimental.pallas import tpu as pltpu
from jax.sharding import Mesh, PartitionSpec as P

HEADS = 36
HEAD_DIM = 64
PAGE = 128
D = HEADS * HEAD_DIM
HP = 48
LW = 128
GROUP = 4
W = D + LW
NEG_FILL = -1e30
NORM_EPS = 1e-06
F32 = jnp.float32
BF16 = jnp.bfloat16


def dot(a, b, ca=1, cb=0):
    return lax.dot_general(a, b, (((ca,), (cb,)), ((), ())), preferred_element_type=F32)


def head_mask(rows, cols):
    row = lax.broadcasted_iota(jnp.int32, (rows, cols), 0)
    col = lax.broadcasted_iota(jnp.int32, (rows, cols), 1)
    return (col >= row * HEAD_DIM) & (col < (row + 1) * HEAD_DIM)


def placed(part, shape, axis):
    head = lax.broadcasted_iota(jnp.int32, shape, axis)
    lane = lax.broadcasted_iota(jnp.int32, shape, 1 - axis)
    return ((lane == head + part * HEADS) & (head < HEADS)).astype(BF16)


def halves(value):
    high = value.astype(BF16)
    return high, (value - high.astype(F32)).astype(BF16)


def packed(lse):
    first = lse.astype(BF16)
    second, third = halves(lse - first.astype(F32))
    return (
        dot(first, placed(0, (HP, LW), 0))
        + dot(second, placed(1, (HP, LW), 0))
        + dot(third, placed(2, (HP, LW), 0))
    ).astype(BF16)


def unpacked(lanes):
    return dot(lanes, placed(0, (LW, HP), 1) + placed(1, (LW, HP), 1) + placed(2, (LW, HP), 1))


def spread_heads():
    return head_mask(HP, D).astype(F32).astype(BF16)


def combined(values, lses, spread):
    peak = lses[0]
    for lse in lses[1:]:
        peak = jnp.maximum(peak, lse)
    shares = [jnp.exp(lse - peak) for lse in lses]
    whole = shares[0]
    for share in shares[1:]:
        whole = whole + share
    total = None
    for share, value in zip(shares, values):
        high, low = halves(share / whole)
        term = (dot(high, spread) + dot(low, spread)) * value.astype(F32)
        total = term if total is None else total + term
    return total, peak + jnp.log(whole)


def wanted_rows(tall, rows, core):
    line = lax.broadcasted_iota(jnp.int32, (tall, rows), 0)
    slot = lax.broadcasted_iota(jnp.int32, (tall, rows), 1)
    k = line % (rows // 2)
    here = 8 * (k // 4) + 4 * jnp.where(line < rows // 2, core, 1 - core) + k % 4
    return line, slot == here


def attn_kernel(
    q_ref, table_ref, len_ref, flag_ref, res_ref, routes_ref, gates_ref, k_hbm, v_hbm,
    own_ref, other_ref, split_ref, kbuf, vbuf, obuf, ksem, vsem,
):
    pages = k_hbm.shape[0]
    rows = q_ref.shape[0]
    for p in range(pages):
        pltpu.make_async_copy(k_hbm.at[p], kbuf.at[p], ksem.at[p]).start()
    for p in range(pages):
        pltpu.make_async_copy(v_hbm.at[p], vbuf.at[p], vsem.at[p]).start()
    core = lax.axis_index("c")
    first = (lax.axis_index("zl") * 2 + core) * pages
    table = table_ref[...]
    line = lax.broadcasted_iota(jnp.int32, table.shape, 0)
    step = lax.broadcasted_iota(jnp.int32, table.shape, 1)
    length = jnp.sum(jnp.where(line == step, len_ref[...].astype(F32), 0.0), axis=1, keepdims=True)
    remain = jnp.clip(length - (step * PAGE).astype(F32), 0.0, float(PAGE))
    lane = lax.broadcasted_iota(jnp.int32, (rows, pages), 1)
    owner = jnp.zeros((rows, pages), F32)
    seen = []
    for p in range(pages):
        match = jnp.where(table == first + p, remain, 0.0)
        per_row = jnp.sum(match, axis=1, keepdims=True)
        seen.append(jnp.sum(per_row, axis=0, keepdims=True).astype(jnp.int32))
        owner = jnp.where((lane == p) & (per_row > 0), 1.0, owner)
    own = res_ref.shape[0]
    spot = lax.broadcasted_iota(jnp.int32, (own, LW), 1)
    square = lax.broadcasted_iota(jnp.int32, (own, own), 0) == lax.broadcasted_iota(jnp.int32, (own, own), 1)
    coefs = jnp.zeros((own, LW), F32)
    for k in range(2):
        route, gate = (
            jnp.sum(jnp.where(square, ref[k : k + 1, :].astype(F32), 0.0), axis=1, keepdims=True)
            for ref in (routes_ref, gates_ref)
        )
        coefs = coefs + jnp.where(spot == route.astype(jnp.int32), gate, 0.0)
    own_ref[rows // 2 : rows // 2 + own, :D] = res_ref[...]
    own_ref[rows // 2 : rows // 2 + own, D:] = coefs.astype(BF16)
    own_ref[rows // 2 + own :, :] = jnp.zeros((own_ref.shape[0] - rows // 2 - own, W), BF16)
    owner_b = owner.astype(BF16)
    q_sel = dot(owner_b, q_ref[...], 0, 0)
    mask = head_mask(HP, D)
    spread = mask.astype(F32).astype(BF16)
    token = lax.broadcasted_iota(jnp.int32, (PAGE, HP), 0)
    tops, sums, weights = [], [], []
    for p0 in range(0, pages, GROUP):
        for p in range(p0, p0 + GROUP):
            pltpu.make_async_copy(k_hbm.at[p], kbuf.at[p], ksem.at[p]).wait()
        for p in range(p0, p0 + GROUP):
            q_diag = jnp.where(mask, q_sel[p : p + 1, :], 0.0).astype(BF16)
            scores = dot(kbuf[p], q_diag, 1, 1) * HEAD_DIM**-0.5
            visible = token < seen[p]
            scores = jnp.where(visible, scores, NEG_FILL)
            top = jnp.max(scores, axis=0, keepdims=True)
            terms = jnp.where(visible, jnp.exp(scores - top), 0.0)
            tops.append(top)
            sums.append(jnp.sum(terms, axis=0, keepdims=True))
            weights.append(terms.astype(BF16))
    for p0 in range(0, pages, GROUP):
        for p in range(p0, p0 + GROUP):
            pltpu.make_async_copy(v_hbm.at[p], vbuf.at[p], vsem.at[p]).wait()
        for p in range(p0, p0 + GROUP):
            mixed = dot(weights[p], vbuf[p], 0, 0)
            obuf[p : p + 1, :] = jnp.sum(jnp.where(mask, mixed, 0.0), axis=0, keepdims=True)
    top = jnp.concatenate(tops, axis=0)
    total = jnp.concatenate(sums, axis=0)
    total = jnp.where(total > 0, total, 1.0)
    lse = top + jnp.log(total)
    same = dot(owner_b, owner_b, 0, 0)
    peak = jnp.full(lse.shape, NEG_FILL, F32)
    for p in range(pages):
        peak = jnp.maximum(peak, jnp.where(same[:, p : p + 1] > 0, lse[p : p + 1, :], NEG_FILL))
    share = jnp.exp(lse - peak)
    whole = jnp.zeros(lse.shape, F32)
    for p in range(pages):
        whole = whole + jnp.where(same[:, p : p + 1] > 0, share[p : p + 1, :], 0.0)
    whole = jnp.where(whole > 0, whole, 1.0)
    high, low = halves(share / (whole * total))
    scaled = (dot(high, spread) + dot(low, spread)) * obuf[...]
    joint = peak + jnp.log(whole)
    half = rows // 2
    tall = rows + split_ref.shape[0]
    line, wanted = wanted_rows(tall, rows, core)
    choice = jnp.where(line < rows, wanted.astype(F32), flag_ref[...].astype(F32))
    chosen = dot(choice.astype(BF16), owner_b)
    chosen_b = chosen.astype(BF16)
    high, low = halves(scaled)
    values = (dot(chosen_b, high) + dot(chosen_b, low)).astype(BF16)
    row_lse = jnp.full((tall, HP), NEG_FILL, F32)
    for p in range(pages):
        row_lse = jnp.maximum(row_lse, jnp.where(chosen[:, p : p + 1] > 0, joint[p : p + 1, :], NEG_FILL))
    lanes = packed(row_lse)
    own_ref[:half, :D] = values[:half, :]
    own_ref[:half, D:] = lanes[:half, :]
    other_ref[:, :D] = values[half:rows, :]
    other_ref[:, D:] = lanes[half:rows, :]
    split_ref[:, :D] = values[rows:, :]
    split_ref[:, D:] = lanes[rows:, :]


def chip_kernel(
    own_ref, other_ref, far_0_ref, far_1_ref, flag_ref, out_ref
):
    half = other_ref.shape[0]
    _, wanted = wanted_rows(half, 2 * half, lax.axis_index("c"))
    flag = jnp.sum(jnp.where(wanted, flag_ref[...].astype(F32), 0.0), axis=1, keepdims=True) > 0
    values = [own_ref[:half, :D], other_ref[:, :D]]
    lses = [unpacked(own_ref[:half, D:]), unpacked(other_ref[:, D:])]
    for far in (far_0_ref, far_1_ref):
        values.append(far[0:1, :D])
        lses.append(jnp.where(flag, unpacked(far[:, D:])[0:1, :], NEG_FILL))
    total, lse = combined(values, lses, spread_heads())
    out_ref[:half, :D] = total.astype(BF16)
    out_ref[:half, D:] = packed(lse)
    out_ref[half:, :] = own_ref[half:, :]


def norm_kernel(p0, p1, p2, p3, gain_ref, attn_ref, out_ref):
    parts = (p0, p1, p2, p3)
    rows = out_ref.shape[0]
    own = attn_ref.shape[0]
    total, _ = combined(
        [part[:rows, :D] for part in parts],
        [unpacked(part[:rows, D:]) for part in parts],
        spread_heads(),
    )
    line = lax.broadcasted_iota(jnp.int32, (rows, rows), 0)
    slot = lax.broadcasted_iota(jnp.int32, (rows, rows), 1)
    source = (lax.axis_index("zl") + 4 - line // own) % 4
    turn = (slot == own * source + line % own).astype(F32).astype(BF16)
    attn = dot(turn, total.astype(BF16))
    attn_ref[...] = attn[:own, :].astype(BF16)
    extra = jnp.concatenate([part[rows : rows + own, :].astype(F32) for part in parts], axis=0)
    stream = extra[:, :D] + attn
    normed = stream * lax.rsqrt(jnp.mean(stream * stream, axis=-1, keepdims=True) + NORM_EPS)
    out_ref[:, :D] = (normed * gain_ref[...].astype(F32)).astype(BF16)
    out_ref[:, D:] = extra[:, D:].astype(BF16)


def hold_kernel(*refs):
    count = len(refs) // 2
    for source, target in zip(refs[:count], refs[count:]):
        target[...] = source[...]


def mlp_kernel(x_ref, gate_0, up_0, down_0, gate_1, up_1, down_1, out_ref):
    x = x_ref[:, :D]
    coefs = x_ref[:, D:].astype(F32)
    lane = lax.broadcasted_iota(jnp.int32, coefs.shape, 1)
    mine = lax.axis_index("zl") * 2 + lax.axis_index("c")
    theirs = lax.axis_index("zl") * 2 + 1 - lax.axis_index("c")
    result = None
    for expert, gate, up, down in ((mine, gate_0, up_0, down_0), (theirs, gate_1, up_1, down_1)):
        coef = jnp.sum(jnp.where(lane == expert, coefs, 0.0), axis=1, keepdims=True)
        g = dot(x, gate[...], 1, 1)
        u = dot(x, up[...], 1, 1)
        inner = ((g / (1.0 + jnp.exp(-g))) * u * coef).astype(BF16)
        y = dot(inner, down[...])
        result = y if result is None else result + y
    out_ref[...] = result.astype(BF16)


def join_kernel(*refs):
    out_ref = refs[-1]
    size = refs[0].shape[0]
    for i, ref in enumerate(refs[:-1]):
        out_ref[size * i : size * (i + 1), :] = ref[...]


def vmem(mib):
    return pltpu.CompilerParams(vmem_limit_bytes=mib * 1024 * 1024)


VMEM_SPEC = pl.BlockSpec(memory_space=pltpu.VMEM)
HBM_SPEC = pl.BlockSpec(memory_space=pl.ANY)
PLANE = ("x", "yh", "yp", "c")


def flipped(array, axis, n=2):
    return lax.ppermute(array, axis, [(i, n - 1 - i) for i in range(n)])


def mirrored(array):
    return lax.ppermute(array, ("zh", "zl"), [(i, 7 - i) for i in range(8)])


def along_line(array, shift, n=4):
    return lax.ppermute(array, "zl", [(i, (i + shift) % n) for i in range(n)])


def along_plane(array, shift, wide, n=4):
    pairs = []
    for x in range(n):
        for y in range(n):
            for c in range(2):
                on_y = (c == 0) == wide
                to_x, to_y = (x, (y + shift) % n) if on_y else ((x + shift) % n, y)
                pairs.append(((x * n + y) * 2 + c, (to_x * n + to_y) * 2 + c))
    return lax.ppermute(array, PLANE, pairs)


def joined(*blocks):
    rows = sum(block.shape[0] for block in blocks)
    return pl.pallas_call(
        join_kernel,
        out_shape=jax.ShapeDtypeStruct((rows, W), BF16),
        compiler_params=vmem(8),
        name="join",
    )(*blocks)


def summed(blocks):
    total = blocks[0].astype(F32)
    for block in blocks[1:]:
        total = total + block.astype(F32)
    return total.astype(BF16)


def pieces(array):
    size = array.shape[0] // 4
    return [array[size * i : size * (i + 1)] for i in range(4)]


NEAR = (1, 3, 2)
WIDE = (2, 3, 1)


def on_device(
    queries, residual, gain, key_pages, value_pages, page_table, lengths, split_flag, routes, gates,
    w_gate, w_up, w_down,
):
    own = residual.shape[0]
    rows = queries.shape[0]
    half = rows // 2
    pages = key_pages.shape[0]
    mine = (w_gate[0].T, w_up[0].T, w_down[0])
    theirs = tuple(flipped(w, "c") for w in mine)
    flag_row = split_flag.reshape(1, rows)

    here, there, split = pl.pallas_call(
        attn_kernel,
        out_shape=(
            jax.ShapeDtypeStruct((half + 8, W), BF16),
            jax.ShapeDtypeStruct((half, W), BF16),
            jax.ShapeDtypeStruct((8, W), BF16),
        ),
        in_specs=[VMEM_SPEC] * 7 + [HBM_SPEC] * 2,
        scratch_shapes=[
            pltpu.VMEM((pages, PAGE, D), BF16),
            pltpu.VMEM((pages, PAGE, D), BF16),
            pltpu.VMEM((pages, D), F32),
            pltpu.SemaphoreType.DMA((pages,)),
            pltpu.SemaphoreType.DMA((pages,)),
        ],
        compiler_params=vmem(60),
        cost_estimate=pl.CostEstimate(flops=2 * 10**9, bytes_accessed=10**7, transcendentals=10**6),
        name="attn",
    )(
        queries, page_table, lengths.reshape(1, rows), flag_row, residual, routes.T, gates.T,
        key_pages, value_pages,
    )
    here, there, split, theirs = lax.optimization_barrier((here, there, split, theirs))
    across = flipped(there, "c")
    far_0 = flipped(split, "yp")
    far_1 = lax.ppermute(split, ("yp", "c"), [(i, 3 - i) for i in range(4)])
    chip = pl.pallas_call(
        chip_kernel,
        out_shape=jax.ShapeDtypeStruct((half + 8, W), BF16),
        compiler_params=vmem(8),
        name="chip",
    )(here, across, far_0, far_1, flag_row)
    chip, mine, theirs = lax.optimization_barrier((chip, mine, theirs))
    weights = pl.pallas_call(
        hold_kernel,
        out_shape=[jax.ShapeDtypeStruct(w.shape, BF16) for w in mine + theirs],
        in_specs=[VMEM_SPEC] * 6,
        compiler_params=vmem(16),
        name="hold",
    )(*mine, *theirs)
    attn, normed = pl.pallas_call(
        norm_kernel,
        out_shape=(jax.ShapeDtypeStruct((own, D), BF16), jax.ShapeDtypeStruct((half, W), BF16)),
        compiler_params=vmem(8),
        name="norm",
    )(chip, *[along_line(chip, s) for s in (1, 2, 3)], gain.reshape(1, D))

    def mlp(block):
        return pl.pallas_call(
            mlp_kernel,
            out_shape=jax.ShapeDtypeStruct((block.shape[0], D), BF16),
            compiler_params=vmem(16),
            cost_estimate=pl.CostEstimate(flops=3 * 10**9, bytes_accessed=10**7, transcendentals=10**5),
            name="mlp",
        )(block, *weights)

    group = joined(normed, mirrored(normed))
    line = joined(group, *[along_plane(group, s, False) for s in NEAR])
    blocks = [along_plane(line, s, True) for s in WIDE]
    first = mlp(line)
    results = [mlp(block) for block in blocks]
    back = [along_plane(result, -s, True) for s, result in zip(WIDE, results)]
    parts = pieces(summed([first] + back))
    total = summed(parts[:1] + [along_plane(part, -s, False) for s, part in zip(NEAR, parts[1:])])
    total = summed([total[:half], mirrored(total[half:])])
    parts = pieces(total)
    return summed(parts[:1] + [along_line(part, -s) for s, part in zip((1, 2, 3), parts[1:])] + [attn])


def solution(mesh):
    fine = Mesh(mesh.devices.reshape(4, 2, 2, 2, 4, 2), ("x", "zh", "yh", "yp", "zl", "c"))
    grp = ("x", "zh", "yh", "yp")
    ep = ("zl", "c")
    in_specs = (
        P(grp, None),
        P(grp + ep, None),
        P(),
        P(grp + ep, None, None),
        P(grp + ep, None, None),
        P(grp, None),
        P(grp),
        P(grp),
        P(grp + ep, None),
        P(grp + ep, None),
        P(ep, None, grp),
        P(ep, None, grp),
        P(ep, grp, None),
    )
    return jax.shard_map(
        on_device, mesh=fine, in_specs=in_specs, out_specs=P(grp + ep, None), check_vma=False
    )
```

```python
import jax
import jax.numpy as jnp
from jax import lax
from jax.experimental import pallas as pl
from jax.experimental.pallas import tpu as pltpu
from jax.sharding import Mesh, PartitionSpec as P

HEADS = 36
HEAD_DIM = 64
PAGE = 128
D = HEADS * HEAD_DIM
HP = 48
LW = 128
GROUP = 4
W = D + LW
CUT = (0, 640, 1280, 1792, 2304)
WX = W + 640
NEG_FILL = -1e30
NORM_EPS = 1e-06
F32 = jnp.float32
BF16 = jnp.bfloat16


def dot(a, b, ca=1, cb=0):
    return lax.dot_general(a, b, (((ca,), (cb,)), ((), ())), preferred_element_type=F32)


def head_mask(rows, cols):
    row = lax.broadcasted_iota(jnp.int32, (rows, cols), 0)
    col = lax.broadcasted_iota(jnp.int32, (rows, cols), 1)
    return (col >= row * HEAD_DIM) & (col < (row + 1) * HEAD_DIM)


def placed(part, shape, axis):
    head = lax.broadcasted_iota(jnp.int32, shape, axis)
    lane = lax.broadcasted_iota(jnp.int32, shape, 1 - axis)
    return ((lane == head + part * HEADS) & (head < HEADS)).astype(BF16)


def halves(value):
    high = value.astype(BF16)
    return high, (value - high.astype(F32)).astype(BF16)


def packed(lse):
    first = lse.astype(BF16)
    second, third = halves(lse - first.astype(F32))
    return (
        dot(first, placed(0, (HP, LW), 0))
        + dot(second, placed(1, (HP, LW), 0))
        + dot(third, placed(2, (HP, LW), 0))
    ).astype(BF16)


def unpacked(lanes):
    return dot(lanes, placed(0, (LW, HP), 1) + placed(1, (LW, HP), 1) + placed(2, (LW, HP), 1))


def spread_heads():
    return head_mask(HP, D).astype(F32).astype(BF16)


def combined(values, lses, spread):
    peak = lses[0]
    for lse in lses[1:]:
        peak = jnp.maximum(peak, lse)
    shares = [jnp.exp(lse - peak) for lse in lses]
    whole = shares[0]
    for share in shares[1:]:
        whole = whole + share
    total = None
    for share, value in zip(shares, values):
        high, low = halves(share / whole)
        term = (dot(high, spread) + dot(low, spread)) * value.astype(F32)
        total = term if total is None else total + term
    return total, peak + jnp.log(whole)


def wanted_rows(tall, rows, core):
    line = lax.broadcasted_iota(jnp.int32, (tall, rows), 0)
    slot = lax.broadcasted_iota(jnp.int32, (tall, rows), 1)
    k = line % (rows // 2)
    here = 8 * (k // 4) + 4 * jnp.where(line < rows // 2, core, 1 - core) + k % 4
    return line, slot == here


def attn_kernel(
    q_ref, table_ref, len_ref, flag_ref, res_ref, routes_ref, gates_ref, k_hbm, v_hbm,
    own_ref, other_ref, split_ref, kbuf, vbuf, obuf, ksem, vsem,
):
    pages = k_hbm.shape[0]
    rows = q_ref.shape[0]
    for p in range(pages):
        pltpu.make_async_copy(k_hbm.at[p], kbuf.at[p], ksem.at[p]).start()
    for p in range(pages):
        pltpu.make_async_copy(v_hbm.at[p], vbuf.at[p], vsem.at[p]).start()
    core = lax.axis_index("c")
    first = (lax.axis_index("zl") * 2 + core) * pages
    table = table_ref[...]
    line = lax.broadcasted_iota(jnp.int32, table.shape, 0)
    step = lax.broadcasted_iota(jnp.int32, table.shape, 1)
    length = jnp.sum(jnp.where(line == step, len_ref[...].astype(F32), 0.0), axis=1, keepdims=True)
    remain = jnp.clip(length - (step * PAGE).astype(F32), 0.0, float(PAGE))
    lane = lax.broadcasted_iota(jnp.int32, (rows, pages), 1)
    owner = jnp.zeros((rows, pages), F32)
    seen = []
    for p in range(pages):
        match = jnp.where(table == first + p, remain, 0.0)
        per_row = jnp.sum(match, axis=1, keepdims=True)
        seen.append(jnp.sum(per_row, axis=0, keepdims=True).astype(jnp.int32))
        owner = jnp.where((lane == p) & (per_row > 0), 1.0, owner)
    own = res_ref.shape[0]
    spot = lax.broadcasted_iota(jnp.int32, (own, LW), 1)
    square = lax.broadcasted_iota(jnp.int32, (own, own), 0) == lax.broadcasted_iota(jnp.int32, (own, own), 1)
    coefs = jnp.zeros((own, LW), F32)
    for k in range(2):
        route, gate = (
            jnp.sum(jnp.where(square, ref[k : k + 1, :].astype(F32), 0.0), axis=1, keepdims=True)
            for ref in (routes_ref, gates_ref)
        )
        coefs = coefs + jnp.where(spot == route.astype(jnp.int32), gate, 0.0)
    extra = None
    line = lax.broadcasted_iota(jnp.int32, (rows // 2, own), 0)
    slot = lax.broadcasted_iota(jnp.int32, (rows // 2, own), 1)
    for q in range(4):
        piece = res_ref[:, CUT[q] : CUT[q + 1]]
        if q == 2:
            piece = jnp.concatenate([piece, coefs.astype(BF16)], axis=1)
        if q == 3:
            piece = jnp.concatenate([piece, jnp.zeros((own, LW), BF16)], axis=1)
        term = dot((line == 4 * slot + q).astype(F32).astype(BF16), piece)
        extra = term if extra is None else extra + term
    own_ref[:, W:] = extra.astype(BF16)
    owner_b = owner.astype(BF16)
    q_sel = dot(owner_b, q_ref[...], 0, 0)
    mask = head_mask(HP, D)
    spread = mask.astype(F32).astype(BF16)
    token = lax.broadcasted_iota(jnp.int32, (PAGE, HP), 0)
    tops, sums, weights = [], [], []
    for p0 in range(0, pages, GROUP):
        for p in range(p0, p0 + GROUP):
            pltpu.make_async_copy(k_hbm.at[p], kbuf.at[p], ksem.at[p]).wait()
        for p in range(p0, p0 + GROUP):
            q_diag = jnp.where(mask, q_sel[p : p + 1, :], 0.0).astype(BF16)
            scores = dot(kbuf[p], q_diag, 1, 1) * HEAD_DIM**-0.5
            visible = token < seen[p]
            scores = jnp.where(visible, scores, NEG_FILL)
            top = jnp.max(scores, axis=0, keepdims=True)
            terms = jnp.where(visible, jnp.exp(scores - top), 0.0)
            tops.append(top)
            sums.append(jnp.sum(terms, axis=0, keepdims=True))
            weights.append(terms.astype(BF16))
    for p0 in range(0, pages, GROUP):
        for p in range(p0, p0 + GROUP):
            pltpu.make_async_copy(v_hbm.at[p], vbuf.at[p], vsem.at[p]).wait()
        for p in range(p0, p0 + GROUP):
            mixed = dot(weights[p], vbuf[p], 0, 0)
            obuf[p : p + 1, :] = jnp.sum(jnp.where(mask, mixed, 0.0), axis=0, keepdims=True)
    top = jnp.concatenate(tops, axis=0)
    total = jnp.concatenate(sums, axis=0)
    total = jnp.where(total > 0, total, 1.0)
    lse = top + jnp.log(total)
    same = dot(owner_b, owner_b, 0, 0)
    peak = jnp.full(lse.shape, NEG_FILL, F32)
    for p in range(pages):
        peak = jnp.maximum(peak, jnp.where(same[:, p : p + 1] > 0, lse[p : p + 1, :], NEG_FILL))
    share = jnp.exp(lse - peak)
    whole = jnp.zeros(lse.shape, F32)
    for p in range(pages):
        whole = whole + jnp.where(same[:, p : p + 1] > 0, share[p : p + 1, :], 0.0)
    whole = jnp.where(whole > 0, whole, 1.0)
    high, low = halves(share / (whole * total))
    scaled = (dot(high, spread) + dot(low, spread)) * obuf[...]
    joint = peak + jnp.log(whole)
    half = rows // 2
    tall = rows + split_ref.shape[0]
    line, wanted = wanted_rows(tall, rows, core)
    choice = jnp.where(line < rows, wanted.astype(F32), flag_ref[...].astype(F32))
    chosen = dot(choice.astype(BF16), owner_b)
    chosen_b = chosen.astype(BF16)
    high, low = halves(scaled)
    values = (dot(chosen_b, high) + dot(chosen_b, low)).astype(BF16)
    row_lse = jnp.full((tall, HP), NEG_FILL, F32)
    for p in range(pages):
        row_lse = jnp.maximum(row_lse, jnp.where(chosen[:, p : p + 1] > 0, joint[p : p + 1, :], NEG_FILL))
    lanes = packed(row_lse)
    own_ref[:, :D] = values[:half, :]
    own_ref[:, D:W] = lanes[:half, :]
    other_ref[:, :D] = values[half:rows, :]
    other_ref[:, D:] = lanes[half:rows, :]
    split_ref[:, :D] = values[rows:, :]
    split_ref[:, D:] = lanes[rows:, :]


def chip_kernel(
    own_ref, other_ref, far_0_ref, far_1_ref, flag_ref, out_ref
):
    half = other_ref.shape[0]
    _, wanted = wanted_rows(half, 2 * half, lax.axis_index("c"))
    flag = jnp.sum(jnp.where(wanted, flag_ref[...].astype(F32), 0.0), axis=1, keepdims=True) > 0
    values = [own_ref[:, :D], other_ref[:, :D]]
    lses = [unpacked(own_ref[:, D:W]), unpacked(other_ref[:, D:])]
    for far in (far_0_ref, far_1_ref):
        values.append(far[0:1, :D])
        lses.append(jnp.where(flag, unpacked(far[:, D:])[0:1, :], NEG_FILL))
    total, lse = combined(values, lses, spread_heads())
    out_ref[:, :D] = total.astype(BF16)
    out_ref[:, D:W] = packed(lse)
    out_ref[:, W:] = own_ref[:, W:]


def norm_kernel(p0, p1, p2, p3, gain_ref, attn_ref, out_ref):
    parts = (p0, p1, p2, p3)
    rows = out_ref.shape[0]
    own = attn_ref.shape[0]
    total, _ = combined(
        [part[:, :D] for part in parts],
        [unpacked(part[:, D:W]) for part in parts],
        spread_heads(),
    )
    line = lax.broadcasted_iota(jnp.int32, (rows, rows), 0)
    slot = lax.broadcasted_iota(jnp.int32, (rows, rows), 1)
    source = (lax.axis_index("zl") + 4 - line // own) % 4
    turn = (slot == own * source + line % own).astype(F32).astype(BF16)
    attn = dot(turn, total.astype(BF16))
    attn_ref[...] = attn[:own, :].astype(BF16)
    extras = jnp.concatenate([part[:, W:] for part in parts], axis=0)
    line = lax.broadcasted_iota(jnp.int32, (rows, 4 * rows), 0)
    slot = lax.broadcasted_iota(jnp.int32, (rows, 4 * rows), 1)
    fetched = [dot((slot == 4 * line + q).astype(F32).astype(BF16), extras) for q in range(4)]
    residual = jnp.concatenate([fetched[q][:, : CUT[q + 1] - CUT[q]] for q in range(4)], axis=1)
    stream = residual + attn
    normed = stream * lax.rsqrt(jnp.mean(stream * stream, axis=-1, keepdims=True) + NORM_EPS)
    out_ref[:, :D] = (normed * gain_ref[...].astype(F32)).astype(BF16)
    out_ref[:, D:] = fetched[2][:, CUT[3] - CUT[2] :].astype(BF16)


def hold_kernel(*refs):
    count = len(refs) // 2
    for source, target in zip(refs[:count], refs[count:]):
        target[...] = source[...]


def mlp_kernel(x_ref, gate_0, up_0, down_0, gate_1, up_1, down_1, out_ref):
    x = x_ref[:, :D]
    coefs = x_ref[:, D:].astype(F32)
    lane = lax.broadcasted_iota(jnp.int32, coefs.shape, 1)
    mine = lax.axis_index("zl") * 2 + lax.axis_index("c")
    theirs = lax.axis_index("zl") * 2 + 1 - lax.axis_index("c")
    result = None
    for expert, gate, up, down in ((mine, gate_0, up_0, down_0), (theirs, gate_1, up_1, down_1)):
        coef = jnp.sum(jnp.where(lane == expert, coefs, 0.0), axis=1, keepdims=True)
        g = dot(x, gate[...], 1, 1)
        u = dot(x, up[...], 1, 1)
        inner = ((g / (1.0 + jnp.exp(-g))) * u * coef).astype(BF16)
        y = dot(inner, down[...])
        result = y if result is None else result + y
    out_ref[...] = result.astype(BF16)


def join_kernel(*refs):
    out_ref = refs[-1]
    size = refs[0].shape[0]
    for i, ref in enumerate(refs[:-1]):
        out_ref[size * i : size * (i + 1), :] = ref[...]


def vmem(mib):
    return pltpu.CompilerParams(vmem_limit_bytes=mib * 1024 * 1024)


VMEM_SPEC = pl.BlockSpec(memory_space=pltpu.VMEM)
HBM_SPEC = pl.BlockSpec(memory_space=pl.ANY)
PLANE = ("x", "yh", "yp", "c")


def flipped(array, axis, n=2):
    return lax.ppermute(array, axis, [(i, n - 1 - i) for i in range(n)])


def mirrored(array):
    return lax.ppermute(array, ("zh", "zl"), [(i, 7 - i) for i in range(8)])


def along_line(array, shift, n=4):
    return lax.ppermute(array, "zl", [(i, (i + shift) % n) for i in range(n)])


def along_plane(array, shift, wide, n=4):
    pairs = []
    for x in range(n):
        for y in range(n):
            for c in range(2):
                on_y = (c == 0) == wide
                to_x, to_y = (x, (y + shift) % n) if on_y else ((x + shift) % n, y)
                pairs.append(((x * n + y) * 2 + c, (to_x * n + to_y) * 2 + c))
    return lax.ppermute(array, PLANE, pairs)


def joined(*blocks):
    rows = sum(block.shape[0] for block in blocks)
    return pl.pallas_call(
        join_kernel,
        out_shape=jax.ShapeDtypeStruct((rows, W), BF16),
        compiler_params=vmem(8),
        name="join",
    )(*blocks)


def summed(blocks):
    total = blocks[0].astype(F32)
    for block in blocks[1:]:
        total = total + block.astype(F32)
    return total.astype(BF16)


def pieces(array):
    size = array.shape[0] // 4
    return [array[size * i : size * (i + 1)] for i in range(4)]


NEAR = (1, 3, 2)
WIDE = (2, 1, 3)


def on_device(
    queries, residual, gain, key_pages, value_pages, page_table, lengths, split_flag, routes, gates,
    w_gate, w_up, w_down,
):
    own = residual.shape[0]
    rows = queries.shape[0]
    half = rows // 2
    pages = key_pages.shape[0]
    mine = (w_gate[0].T, w_up[0].T, w_down[0])
    theirs = tuple(flipped(w, "c") for w in mine)
    flag_row = split_flag.reshape(1, rows)

    here, there, split = pl.pallas_call(
        attn_kernel,
        out_shape=(
            jax.ShapeDtypeStruct((half, WX), BF16),
            jax.ShapeDtypeStruct((half, W), BF16),
            jax.ShapeDtypeStruct((8, W), BF16),
        ),
        in_specs=[VMEM_SPEC] * 7 + [HBM_SPEC] * 2,
        scratch_shapes=[
            pltpu.VMEM((pages, PAGE, D), BF16),
            pltpu.VMEM((pages, PAGE, D), BF16),
            pltpu.VMEM((pages, D), F32),
            pltpu.SemaphoreType.DMA((pages,)),
            pltpu.SemaphoreType.DMA((pages,)),
        ],
        compiler_params=vmem(60),
        cost_estimate=pl.CostEstimate(flops=2 * 10**9, bytes_accessed=10**7, transcendentals=10**6),
        name="attn",
    )(
        queries, page_table, lengths.reshape(1, rows), flag_row, residual, routes.T, gates.T,
        key_pages, value_pages,
    )
    here, there, split, theirs = lax.optimization_barrier((here, there, split, theirs))
    across = flipped(there, "c")
    far_0 = flipped(split, "yp")
    far_1 = lax.ppermute(split, ("yp", "c"), [(i, 3 - i) for i in range(4)])
    chip = pl.pallas_call(
        chip_kernel,
        out_shape=jax.ShapeDtypeStruct((half, WX), BF16),
        compiler_params=vmem(8),
        name="chip",
    )(here, across, far_0, far_1, flag_row)
    chip, mine, theirs = lax.optimization_barrier((chip, mine, theirs))
    weights = pl.pallas_call(
        hold_kernel,
        out_shape=[jax.ShapeDtypeStruct(w.shape, BF16) for w in mine + theirs],
        in_specs=[VMEM_SPEC] * 6,
        compiler_params=vmem(16),
        name="hold",
    )(*mine, *theirs)
    attn, normed = pl.pallas_call(
        norm_kernel,
        out_shape=(jax.ShapeDtypeStruct((own, D), BF16), jax.ShapeDtypeStruct((half, W), BF16)),
        compiler_params=vmem(8),
        name="norm",
    )(chip, *[along_line(chip, s) for s in (1, 2, 3)], gain.reshape(1, D))

    def mlp(block):
        return pl.pallas_call(
            mlp_kernel,
            out_shape=jax.ShapeDtypeStruct((block.shape[0], D), BF16),
            compiler_params=vmem(16),
            cost_estimate=pl.CostEstimate(flops=3 * 10**9, bytes_accessed=10**7, transcendentals=10**5),
            name="mlp",
        )(block, *weights)

    group = joined(normed, mirrored(normed))
    line = joined(group, *[along_plane(group, s, False) for s in NEAR])
    blocks = [along_plane(line, s, True) for s in WIDE]
    first = mlp(line)
    results = [mlp(block) for block in blocks]
    back = [along_plane(result, -s, True) for s, result in zip(WIDE, results)]
    parts = pieces(summed([first] + back))
    total = summed(parts[:1] + [along_plane(part, -s, False) for s, part in zip(NEAR, parts[1:])])
    total = summed([total[:half], mirrored(total[half:])])
    parts = pieces(total)
    return summed(parts[:1] + [along_line(part, -s) for s, part in zip((1, 2, 3), parts[1:])] + [attn])


def solution(mesh):
    fine = Mesh(mesh.devices.reshape(4, 2, 2, 2, 4, 2), ("x", "zh", "yh", "yp", "zl", "c"))
    grp = ("x", "zh", "yh", "yp")
    ep = ("zl", "c")
    in_specs = (
        P(grp, None),
        P(grp + ep, None),
        P(),
        P(grp + ep, None, None),
        P(grp + ep, None, None),
        P(grp, None),
        P(grp),
        P(grp),
        P(grp + ep, None),
        P(grp + ep, None),
        P(ep, None, grp),
        P(ep, None, grp),
        P(ep, grp, None),
    )
    return jax.shard_map(
        on_device, mesh=fine, in_specs=in_specs, out_specs=P(grp + ep, None), check_vma=False
    )
```

```python
import jax
import jax.numpy as jnp
from jax import lax
from jax.experimental import pallas as pl
from jax.experimental.pallas import tpu as pltpu
from jax.sharding import Mesh, PartitionSpec as P

HEADS = 36
HEAD_DIM = 64
PAGE = 128
D = HEADS * HEAD_DIM
HP = 48
LW = 128
GROUP = 4
W = D + LW
CUT = (0, 640, 1280, 1792, 2304)
WX = W + 640
NEG_FILL = -1e30
NORM_EPS = 1e-06
F32 = jnp.float32
BF16 = jnp.bfloat16


def dot(a, b, ca=1, cb=0):
    return lax.dot_general(a, b, (((ca,), (cb,)), ((), ())), preferred_element_type=F32)


def head_mask(rows, cols):
    row = lax.broadcasted_iota(jnp.int32, (rows, cols), 0)
    col = lax.broadcasted_iota(jnp.int32, (rows, cols), 1)
    return (col >= row * HEAD_DIM) & (col < (row + 1) * HEAD_DIM)


def placed(part, shape, axis):
    head = lax.broadcasted_iota(jnp.int32, shape, axis)
    lane = lax.broadcasted_iota(jnp.int32, shape, 1 - axis)
    return ((lane == head + part * HEADS) & (head < HEADS)).astype(BF16)


def halves(value):
    high = value.astype(BF16)
    return high, (value - high.astype(F32)).astype(BF16)


def packed(lse):
    first = lse.astype(BF16)
    second, third = halves(lse - first.astype(F32))
    return (
        dot(first, placed(0, (HP, LW), 0))
        + dot(second, placed(1, (HP, LW), 0))
        + dot(third, placed(2, (HP, LW), 0))
    ).astype(BF16)


def unpacked(lanes):
    return dot(lanes, placed(0, (LW, HP), 1) + placed(1, (LW, HP), 1) + placed(2, (LW, HP), 1))


def spread_heads():
    return head_mask(HP, D).astype(F32).astype(BF16)


def combined(values, lses, spread):
    peak = lses[0]
    for lse in lses[1:]:
        peak = jnp.maximum(peak, lse)
    shares = [jnp.exp(lse - peak) for lse in lses]
    whole = shares[0]
    for share in shares[1:]:
        whole = whole + share
    total = None
    for share, value in zip(shares, values):
        high, low = halves(share / whole)
        term = (dot(high, spread) + dot(low, spread)) * value.astype(F32)
        total = term if total is None else total + term
    return total, peak + jnp.log(whole)


def wanted_rows(tall, rows, core):
    line = lax.broadcasted_iota(jnp.int32, (tall, rows), 0)
    slot = lax.broadcasted_iota(jnp.int32, (tall, rows), 1)
    k = line % (rows // 2)
    here = 8 * (k // 4) + 4 * jnp.where(line < rows // 2, core, 1 - core) + k % 4
    return line, slot == here


def attn_kernel(
    q_ref, table_ref, len_ref, flag_ref, res_ref, routes_ref, gates_ref, k_hbm, v_hbm,
    own_ref, other_ref, split_ref, kbuf, vbuf, obuf, ksem, vsem,
):
    pages = k_hbm.shape[0]
    rows = q_ref.shape[0]
    for p in range(pages):
        pltpu.make_async_copy(k_hbm.at[p], kbuf.at[p], ksem.at[p]).start()
    for p in range(pages):
        pltpu.make_async_copy(v_hbm.at[p], vbuf.at[p], vsem.at[p]).start()
    core = lax.axis_index("c")
    first = (lax.axis_index("zl") * 2 + core) * pages
    table = table_ref[...]
    line = lax.broadcasted_iota(jnp.int32, table.shape, 0)
    step = lax.broadcasted_iota(jnp.int32, table.shape, 1)
    length = jnp.sum(jnp.where(line == step, len_ref[...].astype(F32), 0.0), axis=1, keepdims=True)
    remain = jnp.clip(length - (step * PAGE).astype(F32), 0.0, float(PAGE))
    lane = lax.broadcasted_iota(jnp.int32, (rows, pages), 1)
    owner = jnp.zeros((rows, pages), F32)
    seen = []
    for p in range(pages):
        match = jnp.where(table == first + p, remain, 0.0)
        per_row = jnp.sum(match, axis=1, keepdims=True)
        seen.append(jnp.sum(per_row, axis=0, keepdims=True).astype(jnp.int32))
        owner = jnp.where((lane == p) & (per_row > 0), 1.0, owner)
    own = res_ref.shape[0]
    spot = lax.broadcasted_iota(jnp.int32, (own, LW), 1)
    square = lax.broadcasted_iota(jnp.int32, (own, own), 0) == lax.broadcasted_iota(jnp.int32, (own, own), 1)
    coefs = jnp.zeros((own, LW), F32)
    for k in range(2):
        route, gate = (
            jnp.sum(jnp.where(square, ref[k : k + 1, :].astype(F32), 0.0), axis=1, keepdims=True)
            for ref in (routes_ref, gates_ref)
        )
        coefs = coefs + jnp.where(spot == route.astype(jnp.int32), gate, 0.0)
    extra = None
    line = lax.broadcasted_iota(jnp.int32, (rows // 2, own), 0)
    slot = lax.broadcasted_iota(jnp.int32, (rows // 2, own), 1)
    for q in range(4):
        piece = res_ref[:, CUT[q] : CUT[q + 1]]
        if q == 2:
            piece = jnp.concatenate([piece, coefs.astype(BF16)], axis=1)
        if q == 3:
            piece = jnp.concatenate([piece, jnp.zeros((own, LW), BF16)], axis=1)
        term = dot((line == 4 * slot + q).astype(F32).astype(BF16), piece)
        extra = term if extra is None else extra + term
    own_ref[:, W:] = extra.astype(BF16)
    owner_b = owner.astype(BF16)
    q_sel = dot(owner_b, q_ref[...], 0, 0)
    mask = head_mask(HP, D)
    spread = mask.astype(F32).astype(BF16)
    token = lax.broadcasted_iota(jnp.int32, (PAGE, HP), 0)
    tops, sums, weights = [], [], []
    for p0 in range(0, pages, GROUP):
        for p in range(p0, p0 + GROUP):
            pltpu.make_async_copy(k_hbm.at[p], kbuf.at[p], ksem.at[p]).wait()
        for p in range(p0, p0 + GROUP):
            q_diag = jnp.where(mask, q_sel[p : p + 1, :], 0.0).astype(BF16)
            scores = dot(kbuf[p], q_diag, 1, 1) * HEAD_DIM**-0.5
            visible = token < seen[p]
            scores = jnp.where(visible, scores, NEG_FILL)
            top = jnp.max(scores, axis=0, keepdims=True)
            terms = jnp.where(visible, jnp.exp(scores - top), 0.0)
            tops.append(top)
            sums.append(jnp.sum(terms, axis=0, keepdims=True))
            weights.append(terms.astype(BF16))
    for p0 in range(0, pages, GROUP):
        for p in range(p0, p0 + GROUP):
            pltpu.make_async_copy(v_hbm.at[p], vbuf.at[p], vsem.at[p]).wait()
        for p in range(p0, p0 + GROUP):
            mixed = dot(weights[p], vbuf[p], 0, 0)
            obuf[p : p + 1, :] = jnp.sum(jnp.where(mask, mixed, 0.0), axis=0, keepdims=True)
    top = jnp.concatenate(tops, axis=0)
    total = jnp.concatenate(sums, axis=0)
    total = jnp.where(total > 0, total, 1.0)
    lse = top + jnp.log(total)
    same = dot(owner_b, owner_b, 0, 0)
    peak = jnp.full(lse.shape, NEG_FILL, F32)
    for p in range(pages):
        peak = jnp.maximum(peak, jnp.where(same[:, p : p + 1] > 0, lse[p : p + 1, :], NEG_FILL))
    share = jnp.exp(lse - peak)
    whole = jnp.zeros(lse.shape, F32)
    for p in range(pages):
        whole = whole + jnp.where(same[:, p : p + 1] > 0, share[p : p + 1, :], 0.0)
    whole = jnp.where(whole > 0, whole, 1.0)
    high, low = halves(share / (whole * total))
    scaled = (dot(high, spread) + dot(low, spread)) * obuf[...]
    joint = peak + jnp.log(whole)
    half = rows // 2
    tall = rows + split_ref.shape[0]
    line, wanted = wanted_rows(tall, rows, core)
    choice = jnp.where(line < rows, wanted.astype(F32), flag_ref[...].astype(F32))
    chosen = dot(choice.astype(BF16), owner_b)
    chosen_b = chosen.astype(BF16)
    high, low = halves(scaled)
    values = (dot(chosen_b, high) + dot(chosen_b, low)).astype(BF16)
    row_lse = jnp.full((tall, HP), NEG_FILL, F32)
    for p in range(pages):
        row_lse = jnp.maximum(row_lse, jnp.where(chosen[:, p : p + 1] > 0, joint[p : p + 1, :], NEG_FILL))
    lanes = packed(row_lse)
    own_ref[:, :D] = values[:half, :]
    own_ref[:, D:W] = lanes[:half, :]
    other_ref[:, :D] = values[half:rows, :]
    other_ref[:, D:] = lanes[half:rows, :]
    split_ref[:, :D] = values[rows:, :]
    split_ref[:, D:] = lanes[rows:, :]


def chip_kernel(
    own_ref, other_ref, far_0_ref, far_1_ref, flag_ref, out_ref
):
    half = other_ref.shape[0]
    _, wanted = wanted_rows(half, 2 * half, lax.axis_index("c"))
    flag = jnp.sum(jnp.where(wanted, flag_ref[...].astype(F32), 0.0), axis=1, keepdims=True) > 0
    values = [own_ref[:, :D], other_ref[:, :D]]
    lses = [unpacked(own_ref[:, D:W]), unpacked(other_ref[:, D:])]
    for far in (far_0_ref, far_1_ref):
        values.append(far[0:1, :D])
        lses.append(jnp.where(flag, unpacked(far[:, D:])[0:1, :], NEG_FILL))
    total, lse = combined(values, lses, spread_heads())
    out_ref[:, :D] = total.astype(BF16)
    out_ref[:, D:W] = packed(lse)
    out_ref[:, W:] = own_ref[:, W:]


def norm_kernel(p0, p1, p2, p3, gain_ref, attn_ref, out_ref):
    parts = (p0, p1, p2, p3)
    rows = out_ref.shape[0]
    own = attn_ref.shape[0]
    total, _ = combined(
        [part[:, :D] for part in parts],
        [unpacked(part[:, D:W]) for part in parts],
        spread_heads(),
    )
    line = lax.broadcasted_iota(jnp.int32, (rows, rows), 0)
    slot = lax.broadcasted_iota(jnp.int32, (rows, rows), 1)
    source = (lax.axis_index("zl") + 4 - line // own) % 4
    turn = (slot == own * source + line % own).astype(F32).astype(BF16)
    attn = dot(turn, total.astype(BF16))
    attn_ref[...] = attn[:own, :].astype(BF16)
    extras = jnp.concatenate([part[:, W:] for part in parts], axis=0)
    line = lax.broadcasted_iota(jnp.int32, (rows, 4 * rows), 0)
    slot = lax.broadcasted_iota(jnp.int32, (rows, 4 * rows), 1)
    fetched = [dot((slot == 4 * line + q).astype(F32).astype(BF16), extras) for q in range(4)]
    residual = jnp.concatenate([fetched[q][:, : CUT[q + 1] - CUT[q]] for q in range(4)], axis=1)
    stream = residual + attn
    normed = stream * lax.rsqrt(jnp.mean(stream * stream, axis=-1, keepdims=True) + NORM_EPS)
    out_ref[:, :D] = (normed * gain_ref[...].astype(F32)).astype(BF16)
    out_ref[:, D:] = fetched[2][:, CUT[3] - CUT[2] :].astype(BF16)


def hold_kernel(*refs):
    count = len(refs) // 2
    for source, target in zip(refs[:count], refs[count:]):
        target[...] = source[...]


def mlp_kernel(x_ref, gate_0, up_0, down_0, gate_1, up_1, down_1, out_ref):
    x = x_ref[:, :D]
    coefs = x_ref[:, D:].astype(F32)
    lane = lax.broadcasted_iota(jnp.int32, coefs.shape, 1)
    mine = lax.axis_index("zl") * 2 + lax.axis_index("c")
    theirs = lax.axis_index("zl") * 2 + 1 - lax.axis_index("c")
    result = None
    for expert, gate, up, down in ((mine, gate_0, up_0, down_0), (theirs, gate_1, up_1, down_1)):
        coef = jnp.sum(jnp.where(lane == expert, coefs, 0.0), axis=1, keepdims=True)
        g = dot(x, gate[...], 1, 1)
        u = dot(x, up[...], 1, 1)
        inner = ((g / (1.0 + jnp.exp(-g))) * u * coef).astype(BF16)
        y = dot(inner, down[...])
        result = y if result is None else result + y
    out_ref[...] = result.astype(BF16)


def join_kernel(*refs):
    out_ref = refs[-1]
    size = refs[0].shape[0]
    for i, ref in enumerate(refs[:-1]):
        out_ref[size * i : size * (i + 1), :] = ref[...]


def vmem(mib):
    return pltpu.CompilerParams(vmem_limit_bytes=mib * 1024 * 1024)


VMEM_SPEC = pl.BlockSpec(memory_space=pltpu.VMEM)
HBM_SPEC = pl.BlockSpec(memory_space=pl.ANY)
PLANE = ("x", "yh", "yp", "c")


def flipped(array, axis, n=2):
    return lax.ppermute(array, axis, [(i, n - 1 - i) for i in range(n)])


def mirrored(array):
    return lax.ppermute(array, ("zh", "zl"), [(i, 7 - i) for i in range(8)])


def along_line(array, shift, n=4):
    return lax.ppermute(array, "zl", [(i, (i + shift) % n) for i in range(n)])


def along_plane(array, shift, wide, n=4):
    pairs = []
    for x in range(n):
        for y in range(n):
            for c in range(2):
                on_y = (c == 0) == wide
                to_x, to_y = (x, (y + shift) % n) if on_y else ((x + shift) % n, y)
                pairs.append(((x * n + y) * 2 + c, (to_x * n + to_y) * 2 + c))
    return lax.ppermute(array, PLANE, pairs)


def joined(*blocks):
    rows = sum(block.shape[0] for block in blocks)
    return pl.pallas_call(
        join_kernel,
        out_shape=jax.ShapeDtypeStruct((rows, W), BF16),
        compiler_params=vmem(8),
        name="join",
    )(*blocks)


def summed(blocks):
    total = blocks[0].astype(F32)
    for block in blocks[1:]:
        total = total + block.astype(F32)
    return total.astype(BF16)


def pieces(array):
    size = array.shape[0] // 4
    return [array[size * i : size * (i + 1)] for i in range(4)]


NEAR = (1, 3, 2)
WIDE = (2, 1, 3)


def on_device(
    queries, residual, gain, key_pages, value_pages, page_table, lengths, split_flag, routes, gates,
    w_gate, w_up, w_down,
):
    own = residual.shape[0]
    rows = queries.shape[0]
    half = rows // 2
    pages = key_pages.shape[0]
    mine = (w_gate[0].T, w_up[0].T, w_down[0])
    theirs = tuple(flipped(w, "c") for w in mine)
    flag_row = split_flag.reshape(1, rows)

    here, there, split = pl.pallas_call(
        attn_kernel,
        out_shape=(
            jax.ShapeDtypeStruct((half, WX), BF16),
            jax.ShapeDtypeStruct((half, W), BF16),
            jax.ShapeDtypeStruct((8, W), BF16),
        ),
        in_specs=[VMEM_SPEC] * 7 + [HBM_SPEC] * 2,
        scratch_shapes=[
            pltpu.VMEM((pages, PAGE, D), BF16),
            pltpu.VMEM((pages, PAGE, D), BF16),
            pltpu.VMEM((pages, D), F32),
            pltpu.SemaphoreType.DMA((pages,)),
            pltpu.SemaphoreType.DMA((pages,)),
        ],
        compiler_params=vmem(60),
        cost_estimate=pl.CostEstimate(flops=2 * 10**9, bytes_accessed=10**7, transcendentals=10**6),
        name="attn",
    )(
        queries, page_table, lengths.reshape(1, rows), flag_row, residual, routes.T, gates.T,
        key_pages, value_pages,
    )
    here, there, split, theirs = lax.optimization_barrier((here, there, split, theirs))
    across = flipped(there, "c")
    far_0 = flipped(split, "yp")
    far_1 = lax.ppermute(split, ("yp", "c"), [(i, 3 - i) for i in range(4)])
    chip = pl.pallas_call(
        chip_kernel,
        out_shape=jax.ShapeDtypeStruct((half, WX), BF16),
        compiler_params=vmem(8),
        name="chip",
    )(here, across, far_0, far_1, flag_row)
    chip, mine, theirs = lax.optimization_barrier((chip, mine, theirs))
    weights = pl.pallas_call(
        hold_kernel,
        out_shape=[jax.ShapeDtypeStruct(w.shape, BF16) for w in mine + theirs],
        in_specs=[VMEM_SPEC] * 6,
        compiler_params=vmem(16),
        name="hold",
    )(*mine, *theirs)
    across_2, across_1, across_3 = (along_line(chip, s) for s in (2, 1, 3))
    lines = (across_1, across_2, across_3)
    attn, normed = pl.pallas_call(
        norm_kernel,
        out_shape=(jax.ShapeDtypeStruct((own, D), BF16), jax.ShapeDtypeStruct((half, W), BF16)),
        compiler_params=vmem(8),
        name="norm",
    )(chip, *lines, gain.reshape(1, D))

    def mlp(block):
        return pl.pallas_call(
            mlp_kernel,
            out_shape=jax.ShapeDtypeStruct((block.shape[0], D), BF16),
            compiler_params=vmem(16),
            cost_estimate=pl.CostEstimate(flops=3 * 10**9, bytes_accessed=10**7, transcendentals=10**5),
            name="mlp",
        )(block, *weights)

    group = joined(normed, mirrored(normed))
    line = joined(group, *[along_plane(group, s, False) for s in NEAR])
    blocks = [along_plane(line, s, True) for s in WIDE]
    first = mlp(line)
    results = [mlp(block) for block in blocks]
    back = [along_plane(result, -s, True) for s, result in zip(WIDE, results)]
    parts = pieces(summed([first] + back))
    total = summed(parts[:1] + [along_plane(part, -s, False) for s, part in zip(NEAR, parts[1:])])
    total = summed([total[:half], mirrored(total[half:])])
    parts = pieces(total)
    return summed(parts[:1] + [along_line(part, -s) for s, part in zip((1, 2, 3), parts[1:])] + [attn])


def solution(mesh):
    fine = Mesh(mesh.devices.reshape(4, 2, 2, 2, 4, 2), ("x", "zh", "yh", "yp", "zl", "c"))
    grp = ("x", "zh", "yh", "yp")
    ep = ("zl", "c")
    in_specs = (
        P(grp, None),
        P(grp + ep, None),
        P(),
        P(grp + ep, None, None),
        P(grp + ep, None, None),
        P(grp, None),
        P(grp),
        P(grp),
        P(grp + ep, None),
        P(grp + ep, None),
        P(ep, None, grp),
        P(ep, None, grp),
        P(ep, grp, None),
    )
    return jax.shard_map(
        on_device, mesh=fine, in_specs=in_specs, out_specs=P(grp + ep, None), check_vma=False
    )
```
